32 devices in a mesh: section: 8 (over z, y), dp: 4 (over x, core).
Axes of the slice: x: 2, y: 2, z: 4, core: 2. Of those that a mesh axis runs over, the one named last changes fastest.
Arguments:
- acts: bfloat16 [8, 2, 256, 6144], P('section', None, 'dp'), may hold values from -6 to 6
- grads_sent: bfloat16 [8, 2, 256, 6144], P('section', None, 'dp'), may hold values from -48 to 48
- replicas: bfloat16 [8, 2, 2, 16, 6144], P('section'), may hold values from -4 to 4
- master: float32 [8, 2, 16, 6144], P('section', None, None, 'dp'), may hold values from -1 to 1
- moment: float32 [8, 2, 16, 6144], P('section', None, None, 'dp'), may hold values from -3 to 3
- second: float32 [8, 2, 16, 6144], P('section', None, None, 'dp'), may hold values from 0.05 to 4
Outputs:
- new_master: float32 [8, 2, 16, 6144], P('section', None, None, 'dp')
- new_moment: float32 [8, 2, 16, 6144], P('section', None, None, 'dp')
- new_second: float32 [8, 2, 16, 6144], P('section', None, None, 'dp')
- new_replicas: bfloat16 [8, 2, 2, 16, 6144], P('section')
The draws below stay inside these ranges and needn't reach their ends.
All inputs are finite; a program needn't handle non-finite values.
Results may differ from the reference program's by a relative error of at most 0.006.
Values may be sent and summed in bfloat16 or wider, within the bound.
A program may use at most 64 MiB of HBM per device.

```python
import math
import jax
import jax.numpy as jnp
from jax import lax

D = 6144
FF = 24576
UNITS = 16
TOKENS = 256
N_SECTION = 8


def block_scale(rng, shape, pieces, low, top_value):
    loudness = 1.0
    for axis_at, blocks in pieces:
        steps = jax.random.uniform(jax.random.fold_in(jax.random.fold_in(rng, 6), axis_at), (blocks,), jnp.float32, low / len(pieces), top_value / len(pieces))
        loudness = loudness * jnp.repeat(jnp.exp(steps), shape[axis_at] // blocks).reshape((-1,) + (1,) * (len(shape) - 1 - axis_at))
    return loudness


def gaussian(stream_key, extent, width, bound, cuts=(), held_as=jnp.bfloat16):
    values = width * jax.random.normal(stream_key, extent, jnp.float32)
    if cuts:
        values = values * block_scale(stream_key, extent, cuts, -0.22, 0.18)
    return jnp.clip(values, -bound, bound).astype(held_as)


def setup_inputs(seed: int = 0) -> dict:
    arg_keys = jax.random.split(jax.random.key(seed), 7)
    acts = gaussian(arg_keys[0], (N_SECTION, 2, TOKENS, D), 1.0, 6.0, ((0, 8), (2, 4)))
    grads_sent = gaussian(arg_keys[1], (N_SECTION, 2, TOKENS, D), 8.0, 48.0, ((0, 8), (2, 4)))
    replicas = gaussian(arg_keys[2], (N_SECTION, 2, 2, UNITS, D), 1.0, 4.0, ((0, 8),))
    master = gaussian(arg_keys[3], (N_SECTION, 2, UNITS, D), 0.25, 1.0, ((0, 8), (3, 4)), jnp.float32)
    moment = gaussian(arg_keys[4], (N_SECTION, 2, UNITS, D), 0.5, 3.0, ((0, 8), (3, 4)), jnp.float32)
    second = jnp.clip(jnp.exp(math.log(4.0) - 4.3820266 * jax.random.uniform(arg_keys[5], (N_SECTION, 2, UNITS, D), jnp.float32) ** block_scale(arg_keys[5], (N_SECTION, 2, UNITS, D), ((0, 8), (3, 4)), -0.2, 0.2)), 0.05, 4.0)
    return {"acts": acts, "grads_sent": grads_sent, "replicas": replicas, "master": master, "moment": moment, "second": second}


def gelu_exact(values):
    return 0.5 * values * (1.0 + lax.erf(values * 0.7071067811865476))

def gelu_slope(values):
    return 0.5 * (1.0 + lax.erf(values * 0.7071067811865476)) + values * jnp.exp(-0.5 * values * values) * 0.3989422804014327

def section_terms(inputs, upstream, w_in, w_out):
    inv_width = 1.0 / D ** 0.5
    inv_hidden = 1.0 / FF ** 0.5
    pre_act = jnp.dot(inputs, w_in.T, preferred_element_type=jnp.float32) * inv_width
    activation = gelu_exact(pre_act).astype(jnp.bfloat16)
    act_grad = jnp.dot(upstream, w_out.T, preferred_element_type=jnp.float32) * inv_hidden
    pre_grad = (act_grad * gelu_slope(pre_act)).astype(jnp.bfloat16)
    term_in = jnp.dot(pre_grad.T, inputs, preferred_element_type=jnp.float32) * inv_width
    term_out = jnp.dot(activation.T, upstream, preferred_element_type=jnp.float32) * inv_hidden
    return jnp.stack([term_in, term_out])

def reference(acts, grads_sent, replicas, master, moment, second):
    sections = N_SECTION

    def per_worker(worker):
        after = (worker + 1) % sections
        before = (worker + sections - 1) % sections
        down_up = lax.dynamic_index_in_dim(grads_sent, after.astype(jnp.int32), 0, keepdims=False)[0]
        up_up = lax.dynamic_index_in_dim(grads_sent, before.astype(jnp.int32), 0, keepdims=False)[1]
        own_acts = lax.dynamic_index_in_dim(acts, worker.astype(jnp.int32), 0, keepdims=False)
        own_weights = lax.dynamic_index_in_dim(replicas, worker.astype(jnp.int32), 0, keepdims=False)
        down_terms = section_terms(own_acts[0], down_up, own_weights[0, 0], own_weights[0, 1])
        up_terms = section_terms(own_acts[1], up_up, own_weights[1, 0], own_weights[1, 1])
        return jnp.stack([down_terms, up_terms])
    workers = jnp.arange(sections, dtype=jnp.int32)
    terms = lax.map(per_worker, workers)
    grad = terms[:, 0] + terms[::-1, 1]
    owner_proj = (workers >= sections // 2).astype(jnp.int32)
    mirrors = (sections - 1 - workers).astype(jnp.int32)
    owned = jnp.stack([grad[workers, owner_proj], grad[mirrors, owner_proj]], axis=1)
    new_moment = 0.9 * moment + 0.1 * owned
    new_second = 0.95 * second + 0.05 * owned * owned
    corrected = new_moment / (1.0 - 0.9 ** 10) / (jnp.sqrt(new_second / (1.0 - 0.95 ** 10)) + 1e-08)
    new_master = master - 0.05 * (corrected + 0.01 * master)
    lower = jnp.minimum(workers, mirrors)
    higher = jnp.maximum(workers, mirrors)
    lower_slot = jnp.where(lower == workers, 0, 1).astype(jnp.int32)
    higher_slot = jnp.where(higher == workers, 0, 1).astype(jnp.int32)
    full_section = jnp.stack([new_master[lower, lower_slot], new_master[higher, higher_slot]], axis=1)
    new_replicas = jnp.stack([full_section, full_section[::-1]], axis=1).astype(jnp.bfloat16)
    return (new_master, new_moment, new_second, new_replicas)
```

```python
import functools
import math

import jax
import jax.numpy as jnp
from jax import lax
from jax.experimental import pallas as pl
from jax.experimental.pallas import tpu as pltpu
from jax.sharding import PartitionSpec as P

FF = 24576

beta_one = 0.9
beta_two = 0.95
adam_eps = 1e-08
learn_rate = 0.05
decay_rate = 0.01
adam_steps = 10.0

MESH = pl.DeviceIdType.MESH
NT = (((1,), (1,)), ((), ()))
NN = (((1,), (0,)), ((), ()))


def gelu_exact(values):
    return 0.5 * values * (1.0 + lax.erf(values * 0.7071067811865476))


def gelu_slope(values):
    return (
        0.5 * (1.0 + lax.erf(values * 0.7071067811865476))
        + values * jnp.exp(-0.5 * values * values) * 0.3989422804014327
    )


def dot(a, b, dims):
    return lax.dot_general(a, b, dims, preferred_element_type=jnp.float32)


class Sems:
    def __init__(self, groups):
        self.base, at = {}, 0
        for name, count in groups:
            self.base[name] = at
            at += count
        self.total = at

    def __call__(self, name, k=0):
        return self.base[name] + k


def sem_plan(groups):
    return Sems(
        [
            ("wout", 2),
            ("pass", 2),
            ("act", 2),
            ("back", 2),
            ("pair", 4),
            ("cross", 4 * groups),
            ("owner", 4),
            ("mirror", 2),
            ("spread", 2 * groups),
            ("twin", 2 * groups),
        ]
    )


def kernel(
    S, N, acts, grads, reps, master, moment, second,
    o_master, o_moment, o_second, o_reps,
    acts_v, ups_v, win_v, wout_v, act_s, act_r, ag_s, ag_r,
    term_v, pair_v, x_s, x_r, own_s, own_r, opt_v, opt_o, rep_v,
    load, send, recv,
):
    G = N // 2
    D = acts.shape[-1]
    C = D // N
    H = D // 2
    half = S // 2
    inv_width = 1.0 / D**0.5
    inv_hidden = 1.0 / FF**0.5
    K = sem_plan(G)
    w = lax.axis_index("section")
    d = lax.axis_index("dp")
    g, core = lax.div(d, 2), lax.rem(d, 2)
    nxt, prv, mir = lax.rem(w + 1, S), lax.rem(w + S - 1, S), S - 1 - w
    upper = w >= half
    twin = (w, g * 2 + 1 - core)
    peers = {r: lax.rem(g + r, G) for r in range(1, G)}
    from_ = {r: lax.rem(g + G - r, G) for r in range(1, G)}

    def cols(n):
        return pl.ds(pl.multiple_of(n * C, 128), C)

    def rc(src, dst, k, dev, kr=None):
        return pltpu.make_async_remote_copy(
            src_ref=src, dst_ref=dst, send_sem=send.at[k],
            recv_sem=recv.at[k if kr is None else kr],
            device_id=dev, device_id_type=MESH,
        )

    barrier = pltpu.get_barrier_semaphore()
    greet = [(nxt, d), (prv, d), (mir, d), (S - 1 - nxt, d), (S - 1 - prv, d), twin]
    greet += [(w, peers[r] * 2 + core) for r in range(1, G)]
    for dev in greet:
        pl.semaphore_signal(barrier, inc=1, device_id=dev, device_id_type=MESH)

    loads = [pltpu.make_async_copy(reps.at[:, 0], win_v, load.at[0])]
    loads += [pltpu.make_async_copy(acts.at[c], acts_v.at[c], load.at[1 + c]) for c in range(2)]
    loads += [pltpu.make_async_copy(grads.at[c], ups_v.at[c], load.at[3 + c]) for c in range(2)]
    loads += [
        pltpu.make_async_copy(ref, opt_v.at[i], load.at[5 + i])
        for i, ref in enumerate((master, moment, second))
    ]
    for copy in loads:
        copy.start()
    pl.semaphore_wait(barrier, len(greet))

    sent = []

    def go(copy):
        copy.start()
        sent.append(copy)
        return copy

    ahead = [(nxt, d), (prv, d)]
    behind = [(prv, d), (nxt, d)]
    mine = pl.ds(pl.multiple_of(core * H, 128), H)
    wout = [
        go(rc(reps.at[c, 1, :, mine], wout_v.at[c, :, mine], K("wout", c), ahead[c]))
        for c in range(2)
    ]

    loads[0].wait()
    pre, act_c = [], []
    for c in range(2):
        loads[1 + c].wait()
        value = dot(win_v[c], acts_v[c], NT) * inv_width
        pre.append(value)
        act_s[c] = gelu_exact(value).astype(jnp.bfloat16)
        act_c.append(go(rc(act_s.at[c], act_r.at[c], K("act", c), ahead[c])))

    def put_term(t, value):
        value = value.astype(jnp.bfloat16)
        for n in range(N):
            term_v[n % 2, t, n // 2] = value[:, n * C : (n + 1) * C]
        return go(rc(term_v.at[1 - core, t], pair_v.at[t], K("pair", t), twin))

    pair = [None] * 4
    cross = [None] * 4
    held = [None] * 4

    def to_peers(t):
        pair[t].wait_recv()
        cross[t] = []
        for r in range(1, G):
            x_s[t, r] = (
                term_v[core, t, peers[r]].astype(jnp.float32)
                + pair_v[t, peers[r]].astype(jnp.float32)
            ).astype(jnp.bfloat16)
            cross[t].append(
                go(rc(x_s.at[t, r], x_r.at[t, r], K("cross", t * G + r), (w, peers[r] * 2 + core)))
            )

    def from_peers(t):
        total = term_v[core, t, g].astype(jnp.float32) + pair_v[t, g].astype(jnp.float32)
        for r in range(1, G):
            cross[t][r - 1].wait_recv()
            total = total + x_r[t, r].astype(jnp.float32)
        return total

    for c in range(2):
        loads[3 + c].wait()
        act_c[c].wait_recv()
        pair[2 + c] = put_term(2 + c, dot(act_r[c], ups_v[c], NN) * inv_hidden)

    passed = []
    for c in range(2):
        wout[c].wait_recv()
        passed.append(go(rc(wout_v.at[c, :, mine], wout_v.at[c, :, mine], K("pass", c), twin)))
    to_peers(2)
    to_peers(3)
    back = []
    for c in range(2):
        passed[c].wait_recv()
        ag_s[c] = dot(wout_v[c], ups_v[c], NT) * inv_hidden
        back.append(go(rc(ag_s.at[c], ag_r.at[c], K("back", c), behind[c])))

    low0, low1 = S - 1 - prv, S - 1 - nxt
    dest0 = jnp.where(prv >= half, prv, low0)
    slot0 = jnp.where(prv >= half, 0, 2)
    dest1 = jnp.where(nxt >= half, nxt, low1)
    slot1 = jnp.where(nxt >= half, 3, 1)
    own_s[2] = from_peers(2).astype(jnp.bfloat16)
    own_s[3] = from_peers(3).astype(jnp.bfloat16)
    out0 = rc(own_s.at[2], own_r.at[slot0], K("owner", 2), (dest0, d), K("owner", slot0))
    out1 = rc(own_s.at[3], own_r.at[slot1], K("owner", 3), (dest1, d), K("owner", slot1))

    @pl.when(dest0 != w)
    def _():
        out0.start()

    @pl.when(dest0 == w)
    def _():
        own_r[2] = own_s[2]

    @pl.when(dest1 != w)
    def _():
        out1.start()

    @pl.when(dest1 == w)
    def _():
        own_r[1] = own_s[3]

    for c in range(2):
        back[c].wait_recv()
        pre_grad = (ag_r[c] * gelu_slope(pre[c])).astype(jnp.bfloat16)
        pair[c] = put_term(c, dot(pre_grad, acts_v[c], NN) * inv_width)

    part = jnp.where(upper, 1, 0)
    mine_c = cols(d)

    def arrival(i):
        return rc(own_s.at[0], own_r.at[i], K("owner", i), (mir, d))

    def block(p, n):
        return rep_v.at[:, p, :, cols(n)]

    def share(p, which):
        here = block(p, d)
        return [rc(here, here, K("twin", which * G), twin)] + [
            rc(here, here, K("spread", which * G + r), (w, peers[r] * 2 + core))
            for r in range(1, G)
        ]

    mirror = [
        rc(rep_v.at[j, part, :, mine_c], rep_v.at[1 - j, part, :, mine_c], K("mirror", j), (mir, d))
        for j in range(2)
    ]
    own_share = share(part, 0)

    def update(owned):
        for j in range(2):
            grad = owned[j]
            master_0 = opt_v[0, j]
            moment_now = beta_one * opt_v[1, j] + (1.0 - beta_one) * grad
            second_now = beta_two * opt_v[2, j] + (1.0 - beta_two) * grad * grad
            corrected = (
                moment_now
                / (1.0 - beta_one**adam_steps)
                / (jnp.sqrt(second_now / (1.0 - beta_two**adam_steps)) + adam_eps)
            )
            master_now = master_0 - learn_rate * (corrected + decay_rate * master_0)
            rep_v[j, part, :, mine_c] = master_now.astype(jnp.bfloat16)
            mirror[j].start()
            opt_o[0, j] = master_now
            opt_o[1, j] = moment_now
            opt_o[2, j] = second_now
        for copy in own_share:
            copy.start()

    for i in range(3):
        loads[5 + i].wait()

    to_peers(0)
    to_peers(1)

    @pl.when(upper)
    def _():
        arrival(0).wait_recv()
        arrival(3).wait_recv()

        @pl.when(w != S - 1)
        def _():
            arrival(1).wait_recv()

        @pl.when(w != half)
        def _():
            arrival(2).wait_recv()

        update(
            [
                own_r[2 * j].astype(jnp.float32) + own_r[2 * j + 1].astype(jnp.float32)
                for j in range(2)
            ]
        )

    in0 = rc(own_s.at[0], own_r.at[1], K("owner", 0), (mir, d), K("owner", 1))
    in1 = rc(own_s.at[1], own_r.at[0], K("owner", 1), (mir, d), K("owner", 0))
    term0 = from_peers(0)
    term1 = from_peers(1)

    @pl.when(upper)
    def _():
        own_s[0] = term0.astype(jnp.bfloat16)
        own_s[1] = term1.astype(jnp.bfloat16)
        in0.start()
        in1.start()

    @pl.when(jnp.logical_not(upper))
    def _():
        arrival(0).wait_recv()
        arrival(1).wait_recv()
        update([term0 + own_r[0].astype(jnp.float32), term1 + own_r[1].astype(jnp.float32)])

    outs = [
        pltpu.make_async_copy(opt_o.at[i], ref, load.at[i])
        for i, ref in enumerate((o_master, o_moment, o_second))
    ]
    for copy in outs:
        copy.start()

    other = 1 - part
    far_share = share(other, 1)

    def forward(p, which):
        for r in range(1, G):
            n = from_[r] * 2 + core
            rc(block(p, n), block(p, n), K("spread", which * G + r), twin).wait_recv()
            go(rc(block(p, n), block(p, n), K("twin", which * G + r), twin))

    def take_far():
        for j in range(2):
            mirror[j].wait_recv()
        for copy in far_share:
            copy.start()

    take_far()
    forward(part, 0)
    forward(other, 1)
    for which, p in ((0, part), (1, other)):
        for r in range(G):
            n = (from_[r] if r else g) * 2 + 1 - core
            rc(block(p, n), block(p, n), K("twin", which * G + r), twin).wait_recv()
    last = pltpu.make_async_copy(rep_v, o_reps, load.at[3])
    last.start()

    for copy in sent + mirror + own_share + far_share:
        copy.wait_send()

    @pl.when(dest0 != w)
    def _():
        out0.wait_send()

    @pl.when(dest1 != w)
    def _():
        out1.wait_send()

    @pl.when(upper)
    def _():
        in0.wait_send()
        in1.wait_send()

    for copy in outs:
        copy.wait()
    last.wait()


def body(S, N, acts, grads_sent, replicas, master, moment, second):
    _, _, T, D = acts.shape
    U = replicas.shape[3]
    C = D // N
    G = N // 2
    bf, f32 = jnp.bfloat16, jnp.float32
    K = sem_plan(G)
    any_spec = pl.BlockSpec(memory_space=pl.ANY)
    outs = pl.pallas_call(
        functools.partial(kernel, S, N),
        out_shape=[
            jax.ShapeDtypeStruct((2, U, C), f32),
            jax.ShapeDtypeStruct((2, U, C), f32),
            jax.ShapeDtypeStruct((2, U, C), f32),
            jax.ShapeDtypeStruct((2, 2, U, D), bf),
        ],
        in_specs=[any_spec] * 6,
        out_specs=[any_spec] * 4,
        scratch_shapes=[
            pltpu.VMEM((2, T, D), bf),
            pltpu.VMEM((2, T, D), bf),
            pltpu.VMEM((2, U, D), bf),
            pltpu.VMEM((2, U, D), bf),
            pltpu.VMEM((2, U, T), bf),
            pltpu.VMEM((2, U, T), bf),
            pltpu.VMEM((2, U, T), f32),
            pltpu.VMEM((2, U, T), f32),
            pltpu.VMEM((2, 4, G, U, C), bf),
            pltpu.VMEM((4, G, U, C), bf),
            pltpu.VMEM((4, G, U, C), bf),
            pltpu.VMEM((4, G, U, C), bf),
            pltpu.VMEM((4, U, C), bf),
            pltpu.VMEM((4, U, C), bf),
            pltpu.VMEM((3, 2, U, C), f32),
            pltpu.VMEM((3, 2, U, C), f32),
            pltpu.VMEM((2, 2, U, D), bf),
            pltpu.SemaphoreType.DMA((8,)),
            pltpu.SemaphoreType.DMA((K.total,)),
            pltpu.SemaphoreType.DMA((K.total,)),
        ],
        compiler_params=pltpu.CompilerParams(collective_id=0, has_side_effects=True),
    )(acts[0], grads_sent[0], replicas[0], master[0], moment[0], second[0])
    return tuple(out[None] for out in outs)


def solution(mesh):
    in_specs = (
        P("section", None, "dp", None),
        P("section", None, "dp", None),
        P("section", None, None, None, None),
        P("section", None, None, "dp"),
        P("section", None, None, "dp"),
        P("section", None, None, "dp"),
    )
    out_specs = (
        P("section", None, None, "dp"),
        P("section", None, None, "dp"),
        P("section", None, None, "dp"),
        P("section", None, None, None, None),
    )
    run = functools.partial(body, mesh.shape["section"], mesh.shape["dp"])
    return jax.shard_map(run, mesh=mesh, in_specs=in_specs, out_specs=out_specs, check_vma=False)
```
